128 devices in a mesh: ctx: 32 (over z, x, core), tp: 4 (over y).
Axes of the slice: x: 4, y: 4, z: 4, core: 2. Of those that a mesh axis runs over, the one named last changes fastest.
Arguments:
- seq_input: bfloat16 [65536, 4096], P('ctx', 'tp'), may hold values from -6 to 6
- in_basis: bfloat16 [65536, 128], P('ctx'), may hold values from -1.75 to 1.75
- out_basis: bfloat16 [65536, 128], P('ctx'), may hold values from -1.75 to 1.75
- step_size: float32 [32, 65536], P('tp', 'ctx'), may hold values from 0 to 0.5, as said below
- log_decay: float32 [32, 65536], P('tp', 'ctx'), may hold values from -1 to 0, as said below
- skip_gain: float32 [32], P('tp'), may hold values from 0.5 to 1.5
- access_counts: int32 [32], P('ctx'), may hold values from 512 to 2048, as said below
- out_cotangent: bfloat16 [65536, 4096], P('ctx', 'tp'), may hold values from -6 to 6
Outputs:
- input_grad: bfloat16 [65536, 4096], P('ctx', 'tp')
- in_basis_grad: float32 [65536, 128], P('ctx')
- out_basis_grad: float32 [65536, 128], P('ctx')
- step_grad: float32 [32, 65536], P('tp', 'ctx')
- decay_grad: float32 [32, 65536], P('tp', 'ctx')
The draws below stay inside these ranges and needn't reach their ends.
Inputs may be any that keep to these rules, and one draw needn't show every extreme that they name: `access_counts`: one index of ctx has exactly 2048 used row slots and another exactly a quarter of 2048. `log_decay`: never positive. `step_size`: Positive.
All inputs are finite; a program needn't handle non-finite values.
Results may differ from the reference program's by a relative error of at most 0.03.
Values sent between devices are 32-bit elements; how exact they have to be, the bound alone decides.
No kernel may reach another device: no remote copies, remote signals or barrier semaphores. Data moves between devices by JAX's collectives and lax.ppermute only.
A program may use at most 192 MiB of HBM per device.

```python
import math
import jax
import jax.numpy as jnp
from jax import lax

H = 32
P_SIZE = 128
N = 128
GROUP = 256
L_DEV = 2048
ENTIRE_LINE_SPOTS = 65536


def head_rates(key):
    shared = jax.random.fold_in(key, 11)
    key_fast, key_quick, key_slow = jax.random.split(shared, 3)
    is_fast = jax.random.uniform(key_fast, (H,)) < 0.5
    quick_rate = jnp.exp(jax.random.uniform(key_quick, (H,), jnp.float32, math.log(1.0 / 50.0), math.log(1.0 / 25.0)))
    slow_rate = jnp.exp(jax.random.uniform(key_slow, (H,), jnp.float32, math.log(0.05), math.log(0.2))) / ENTIRE_LINE_SPOTS
    return jnp.where(is_fast, quick_rate, slow_rate)


def draw_log_decay(key, part):
    fading_speeds = head_rates(key)
    own = jax.random.fold_in(key, 21)
    key_rough, key_block, position_seed_handle, layer_seed_handle = jax.random.split(own, 4)
    rough_sample = jnp.exp(jax.random.uniform(key_rough, (H, ENTIRE_LINE_SPOTS), jnp.float32, math.log(0.5), math.log(2.0)))
    segment_factor = jnp.exp(jax.random.uniform(key_block, (H, ENTIRE_LINE_SPOTS // GROUP), jnp.float32, math.log(0.5), math.log(2.0)))
    segment_factor = jnp.repeat(segment_factor, GROUP, axis=1)
    spurt_line_places = jax.random.randint(position_seed_handle, (2,), 0, ENTIRE_LINE_SPOTS)
    spurt_span_number = jax.random.uniform(layer_seed_handle, (2,), jnp.float32, 0.22, 0.69)
    visit_tally = (jnp.arange(ENTIRE_LINE_SPOTS)[None, :] == spurt_line_places[:, None]).astype(jnp.float32)
    spurt_clusters = jnp.sum(visit_tally * spurt_span_number[:, None], axis=0)
    return -fading_speeds[:, None] * rough_sample * segment_factor - spurt_clusters[None, :]


def draw_step_size(key, part):
    fading_speeds = head_rates(key)
    own = jax.random.fold_in(key, 31)
    rough_sample = jnp.exp(jax.random.uniform(own, (H, ENTIRE_LINE_SPOTS), jnp.float32, math.log(0.5), math.log(2.0)))
    return jnp.sqrt(fading_speeds)[:, None] * rough_sample


def draw_access_counts(key, part):
    own = jax.random.fold_in(key, 41)
    key_count, key_order = jax.random.split(own)
    shards = ENTIRE_LINE_SPOTS // L_DEV
    counts = jax.random.randint(key_count, (shards,), L_DEV // 4, L_DEV + 1)
    order = jax.random.permutation(key_order, shards)
    counts = counts.at[order[0]].set(L_DEV)
    counts = counts.at[order[1]].set(L_DEV // 4)
    return counts.astype(jnp.int32)


def block_scale(key, shape, cuts, low, high):
    level, own = 1.0, jax.random.fold_in(key, 6)
    for dim, shards_of in cuts:
        draws = jnp.exp(jax.random.uniform(jax.random.fold_in(own, dim), (shards_of,), jnp.float32, low / len(cuts), high / len(cuts)))
        level = level * jnp.repeat(draws, shape[dim] // shards_of).reshape([-1 if axis == dim else 1 for axis in range(len(shape))])
    return level


def normal_values(rng, dims, width, most, cuts=(), held_as=jnp.bfloat16):
    array = width * jax.random.normal(rng, dims, jnp.float32)
    if cuts:
        array = array * block_scale(rng, dims, cuts, -0.22, 0.18)
    return jnp.clip(array, -most, most).astype(held_as)


def setup_inputs(seed: int = 0) -> dict:
    seeds = jax.random.split(jax.random.key(seed), 9)
    return {
        "seq_input": normal_values(seeds[0], (ENTIRE_LINE_SPOTS, H * P_SIZE), 1.0, 6.0, ((0, 32), (1, 4))),
        "in_basis": normal_values(seeds[1], (ENTIRE_LINE_SPOTS, N), 0.3, 1.75, ((0, 32),)),
        "out_basis": normal_values(seeds[2], (ENTIRE_LINE_SPOTS, N), 0.3, 1.75, ((0, 32),)),
        "step_size": draw_step_size(jax.random.fold_in(seeds[8], 71), 0),
        "log_decay": draw_log_decay(jax.random.fold_in(seeds[8], 71), 0),
        "skip_gain": jnp.clip(0.5 + 1.0 * jax.random.uniform(seeds[5], (H,), jnp.float32) ** block_scale(seeds[5], (H,), ((0, 4),), -0.2, 0.2), 0.5, 1.5),
        "access_counts": draw_access_counts(jax.random.fold_in(seeds[8], 71), 0),
        "out_cotangent": normal_values(seeds[7], (ENTIRE_LINE_SPOTS, H * P_SIZE), 1.0, 6.0, ((0, 32), (1, 4))),
    }


def run_groups(inputs, basis_in, basis_out, step, decay, gain, used, start, block):
    row_count, head_count, head_width = inputs.shape
    blocks = row_count // block
    x_blocks = inputs.reshape(blocks, block, head_count, head_width)
    in_blocks = basis_in.reshape(blocks, block, basis_in.shape[1])
    out_blocks = basis_out.reshape(blocks, block, basis_out.shape[1])
    step_blocks = step.reshape(head_count, blocks, block).transpose(1, 0, 2)
    decay_blocks = decay.reshape(head_count, blocks, block).transpose(1, 0, 2)
    used_blocks = used.reshape(blocks, block)
    later = lax.broadcasted_iota(jnp.int32, (block, block), 0)
    earlier = lax.broadcasted_iota(jnp.int32, (block, block), 1)
    lower_tri = later >= earlier

    @jax.checkpoint
    def advance(state, pieces):
        x_block, in_block, out_block, step_block, decay_block, used_block = pieces
        in_half = in_block.astype(jnp.bfloat16)
        out_half = out_block.astype(jnp.bfloat16)
        cumulative = jnp.cumsum(decay_block, axis=1)
        gaps = jnp.where(lower_tri[None], cumulative[:, :, None] - cumulative[:, None, :], 0.0)
        scores = jnp.dot(out_half, in_half.T, preferred_element_type=jnp.float32)
        weights = (jnp.where(lower_tri[None], jnp.exp(gaps), 0.0) * scores[None]).astype(jnp.bfloat16)
        inject = (x_block * step_block.T[:, :, None]).astype(jnp.bfloat16)
        inner = jnp.einsum('hij,jhp->ihp', weights, inject, preferred_element_type=jnp.float32)
        carried = jnp.einsum('hpn,in->ihp', state.astype(jnp.bfloat16), out_half, preferred_element_type=jnp.float32) * jnp.exp(cumulative).T[:, :, None]
        mixed = (inner + carried + gain[None, :, None] * x_block) * used_block[:, None, None]
        tail_decay = jnp.exp(cumulative[:, -1:] - cumulative)
        scaled = (inject.astype(jnp.float32) * tail_decay.T[:, :, None]).astype(jnp.bfloat16)
        new_state = jnp.exp(cumulative[:, -1])[:, None, None] * state + jnp.einsum('jhp,jn->hpn', scaled, in_half, preferred_element_type=jnp.float32)
        return (new_state, mixed)
    final, mixed_blocks = lax.scan(advance, start, (x_blocks, in_blocks, out_blocks, step_blocks, decay_blocks, used_blocks))
    return (mixed_blocks.reshape(row_count, head_count, head_width), final)

def reference(seq_input, in_basis, out_basis, step_size, log_decay, skip_gain, access_counts, out_cotangent):
    positions = jnp.arange(ENTIRE_LINE_SPOTS, dtype=jnp.int32)
    owner = (positions // L_DEV).astype(jnp.int32)
    used = (positions % L_DEV < access_counts[owner]).astype(jnp.float32)
    inputs = seq_input.astype(jnp.float32).reshape(ENTIRE_LINE_SPOTS, H, P_SIZE)
    basis_in = in_basis.astype(jnp.float32)
    basis_out = out_basis.astype(jnp.float32)
    cotangent = out_cotangent.astype(jnp.float32).reshape(ENTIRE_LINE_SPOTS, H, P_SIZE)
    start = jnp.zeros((H, P_SIZE, N), jnp.float32)

    def forward(x_value, in_value, out_value, step_value, decay_value):
        mixed, final = run_groups(x_value, in_value, out_value, step_value * used[None], decay_value * used[None], skip_gain, used, start, GROUP)
        return mixed
    mixed, pull = jax.vjp(forward, inputs, basis_in, basis_out, step_size, log_decay)
    grad_x, grad_in, grad_out, grad_step, grad_decay = pull(cotangent)
    return (grad_x.reshape(ENTIRE_LINE_SPOTS, H * P_SIZE).astype(jnp.bfloat16), grad_in, grad_out, grad_step, grad_decay)
```

```python
import jax
import jax.numpy as jnp
from jax import lax
from jax.experimental import pallas as pl
from jax.experimental.pallas import tpu as pltpu
from jax.sharding import PartitionSpec as P

L = 256
F32 = jnp.float32
BF16 = jnp.bfloat16
VMEM_LIMIT = 56 * 1024 * 1024


def mm(a, b, ca, cb):
    return lax.dot_general(a, b, (((ca,), (cb,)), ((), ())), preferred_element_type=F32)


def running(rows, reverse):
    j = lax.broadcasted_iota(jnp.int32, (L, L), 0)
    i = lax.broadcasted_iota(jnp.int32, (L, L), 1)
    tri = ((j >= i) if reverse else (j <= i)).astype(F32)
    return lax.dot_general(
        rows, tri, (((1,), (0,)), ((), ())),
        precision=lax.Precision.HIGHEST, preferred_element_type=F32,
    )


def spread(v, width):
    return jnp.concatenate(
        [jnp.broadcast_to(v[h : h + 1, :], (1, width)) for h in range(v.shape[0])], axis=1
    )


def states_kernel(
    count, x_ref, g_ref, b_ref, c_ref, step_ref, decay_ref,
    cum_ref, col_ref, s_ref, a_ref, send_ref, s_acc, a_acc, tot,
):
    heads = step_ref.shape[0]
    blocks = step_ref.shape[1] // L
    width = x_ref.shape[1] // heads
    k = pl.program_id(0)

    @pl.when(k == 0)
    def _():
        s_acc[...] = jnp.zeros_like(s_acc)
        a_acc[...] = jnp.zeros_like(a_acc)
        for n in range(blocks):
            sl = pl.ds(n * L, L)
            at = n * L + lax.broadcasted_iota(jnp.int32, (heads, L), 1)
            used = (at < count[0]).astype(F32)
            st = step_ref[:, sl] * used
            cum = running(decay_ref[:, sl] * used, False)
            cum_ref[:, sl] = cum
            total = cum[:, L - 1 :]
            tot[n] = jnp.broadcast_to(total, (heads, 128))
            rows = jnp.concatenate(
                [st, jnp.exp(cum) * used, jnp.exp(total - cum), cum, used,
                 jnp.zeros((128 - 5 * heads, L), F32)], axis=0
            )
            col_ref[sl, :] = rows.T

    s_ref[0] = s_acc[...]
    rows = pl.ds(pl.multiple_of(k * L, L), L)
    parts = []
    for h in range(heads):
        cs = slice(h * width, (h + 1) * width)
        u = (x_ref[:, cs].astype(F32) * col_ref[rows, h : h + 1]).astype(BF16)
        e = col_ref[rows, 2 * heads + h : 2 * heads + h + 1]
        parts.append((u.astype(F32) * e).astype(BF16))
    scaled = jnp.concatenate(parts, axis=1)
    s_new = spread(jnp.exp(tot[k][:, :1]), width) * s_acc[...] + mm(b_ref[...].T, scaled, 1, 0)
    s_acc[...] = s_new

    back = blocks - 1 - k
    a_ref[0] = a_acc[...]
    rows = pl.ds(pl.multiple_of(back * L, L), L)
    parts = []
    for h in range(heads):
        cs = slice(h * width, (h + 1) * width)
        e = col_ref[rows, heads + h : heads + h + 1]
        parts.append((g_ref[:, cs].astype(F32) * e).astype(BF16))
    dq = jnp.concatenate(parts, axis=1)
    a_new = spread(jnp.exp(tot[back][:, :1]), width) * a_acc[...] + mm(c_ref[...].T, dq, 1, 0)
    a_acc[...] = a_new

    @pl.when(k == blocks - 1)
    def _():
        whole = tot[0]
        for n in range(1, blocks):
            whole = whole + tot[n]
        d = jnp.exp(whole)
        n_dev = send_ref.shape[0]
        each = s_acc.shape[0] // n_dev
        for i in range(n_dev):
            send_ref[i, 2 * each] = d
            for h in range(heads):
                cs = slice(h * width, (h + 1) * width)
                send_ref[i, 0:each, h, :] = s_acc[i * each : (i + 1) * each, cs]
                send_ref[i, each : 2 * each, h, :] = a_acc[i * each : (i + 1) * each, cs]


def local_states(count, x, g, b, c, step, decay, devices):
    heads, rows = step.shape
    blocks = rows // L
    n = b.shape[1]
    wide = x.shape[1]
    each = n // devices
    fwd = lambda k: (k, 0)
    rev = lambda k: (blocks - 1 - k, 0)
    whole = lambda k: (0, 0)
    return pl.pallas_call(
        states_kernel,
        grid=(blocks,),
        in_specs=[
            pl.BlockSpec(memory_space=pltpu.SMEM),
            pl.BlockSpec((L, wide), fwd),
            pl.BlockSpec((L, wide), rev),
            pl.BlockSpec((L, n), fwd),
            pl.BlockSpec((L, n), rev),
            pl.BlockSpec((heads, rows), whole),
            pl.BlockSpec((heads, rows), whole),
        ],
        out_specs=[
            pl.BlockSpec((heads, rows), whole),
            pl.BlockSpec((rows, 128), whole),
            pl.BlockSpec((1, n, wide), lambda k: (k, 0, 0)),
            pl.BlockSpec((1, n, wide), lambda k: (blocks - 1 - k, 0, 0)),
            pl.BlockSpec((devices, 2 * each + 1, heads, 128), lambda k: (0, 0, 0, 0)),
        ],
        out_shape=[
            jax.ShapeDtypeStruct((heads, rows), F32),
            jax.ShapeDtypeStruct((rows, 128), F32),
            jax.ShapeDtypeStruct((blocks, n, wide), F32),
            jax.ShapeDtypeStruct((blocks, n, wide), F32),
            jax.ShapeDtypeStruct((devices, 2 * each + 1, heads, 128), F32),
        ],
        scratch_shapes=[
            pltpu.VMEM((n, wide), F32),
            pltpu.VMEM((n, wide), F32),
            pltpu.VMEM((blocks, heads, 128), F32),
        ],
        compiler_params=pltpu.CompilerParams(vmem_limit_bytes=VMEM_LIMIT),
        name="local_states",
    )(count, x, g, b, c, step, decay)


def scan_kernel(got_ref, out_ref):
    devices, parts = got_ref.shape[0], got_ref.shape[1]
    each = (parts - 1) // 2
    zero = jnp.zeros((each,) + got_ref.shape[2:], F32)
    s = zero
    a = zero
    for i in range(devices):
        out_ref[i, 0:each] = s
        s = got_ref[i, 2 * each][None] * s + got_ref[i, 0:each]
        r = devices - 1 - i
        out_ref[r, each : 2 * each] = a
        a = got_ref[r, 2 * each][None] * a + got_ref[r, each : 2 * each]


def scan_devices(got):
    devices, parts, heads, lanes = got.shape
    return pl.pallas_call(
        scan_kernel,
        out_shape=jax.ShapeDtypeStruct((devices, parts - 1, heads, lanes), F32),
        compiler_params=pltpu.CompilerParams(vmem_limit_bytes=VMEM_LIMIT),
        name="scan_devices",
    )(got)


def inner_kernel(x_ref, g_ref, b_ref, c_ref, cum_ref, col_ref,
                 du_ref, db_ref, dc_ref, q_ref, r_ref):
    heads = cum_ref.shape[0]
    width = x_ref.shape[1] // heads
    b = b_ref[...]
    c = c_ref[...]
    score = mm(b, c, 1, 1)
    j = lax.broadcasted_iota(jnp.int32, (L, L), 0)
    i = lax.broadcasted_iota(jnp.int32, (L, L), 1)
    keep = j <= i
    used = col_ref[:, 4 * heads : 4 * heads + 1]
    lane = lax.broadcasted_iota(jnp.int32, (L, 128), 1)
    dscore = jnp.zeros((L, L), F32)
    r_all = jnp.zeros((L, 128), F32)
    for h in range(heads):
        cs = slice(h * width, (h + 1) * width)
        dy = (g_ref[:, cs].astype(F32) * used).astype(BF16)
        u = (x_ref[:, cs].astype(F32) * col_ref[:, h : h + 1]).astype(BF16)
        gap = cum_ref[h : h + 1, :] - col_ref[:, 3 * heads + h : 3 * heads + h + 1]
        fade = jnp.exp(jnp.where(keep, gap, -1e30))
        w = (fade * score).astype(BF16)
        dw = mm(u, dy, 1, 1)
        dscore = dscore + dw * fade
        prod = dw * w.astype(F32)
        q_ref[h : h + 1, :] = jnp.sum(prod, axis=0, keepdims=True)
        r_all = jnp.where(lane == h, jnp.sum(prod, axis=1, keepdims=True), r_all)
        du_ref[:, cs] = mm(w, dy, 1, 0).astype(BF16)
    r_ref[...] = r_all
    ds = dscore.astype(BF16)
    db_ref[...] = mm(ds, c, 1, 0)
    dc_ref[...] = mm(ds.T, b, 1, 0)


def within(x, g, b, c, cum, col):
    heads, rows = cum.shape
    blocks = rows // L
    n = b.shape[1]
    wide = x.shape[1]
    fwd = lambda k: (k, 0)
    return pl.pallas_call(
        inner_kernel,
        grid=(blocks,),
        in_specs=[
            pl.BlockSpec((L, wide), fwd),
            pl.BlockSpec((L, wide), fwd),
            pl.BlockSpec((L, n), fwd),
            pl.BlockSpec((L, n), fwd),
            pl.BlockSpec((heads, L), lambda k: (0, k)),
            pl.BlockSpec((L, 128), fwd),
        ],
        out_specs=[
            pl.BlockSpec((L, wide), fwd),
            pl.BlockSpec((L, n), fwd),
            pl.BlockSpec((L, n), fwd),
            pl.BlockSpec((heads, L), lambda k: (0, k)),
            pl.BlockSpec((L, 128), fwd),
        ],
        out_shape=[
            jax.ShapeDtypeStruct((rows, wide), BF16),
            jax.ShapeDtypeStruct((rows, n), F32),
            jax.ShapeDtypeStruct((rows, n), F32),
            jax.ShapeDtypeStruct((heads, rows), F32),
            jax.ShapeDtypeStruct((rows, 128), F32),
        ],
        compiler_params=pltpu.CompilerParams(vmem_limit_bytes=VMEM_LIMIT),
        name="within_blocks",
    )(x, g, b, c, cum, col)


def outer_kernel(count, gain, x_ref, g_ref, b_ref, c_ref, cum_ref, col_ref, s_ref, a_ref, got_ref,
                 du_ref, db1_ref, dc1_ref, q_ref, r_ref,
                 dx_ref, db_ref, dc_ref, dstep_ref, ddecay_ref, s0, a0):
    heads = cum_ref.shape[0]
    blocks = cum_ref.shape[1] // L
    width = x_ref.shape[1] // heads
    n = b_ref.shape[1]
    k = pl.program_id(0)
    each = got_ref.shape[1] // 2

    @pl.when(k == 0)
    def _():
        for h in range(heads):
            cs = slice(h * width, (h + 1) * width)
            s0[:, cs] = got_ref[:, 0:each, h, :].reshape(n, width)
            a0[:, cs] = got_ref[:, each : 2 * each, h, :].reshape(n, width)

    before = jnp.zeros((heads, 1), F32)
    after = jnp.zeros((heads, 1), F32)
    own = jnp.zeros((heads, 1), F32)
    for m in range(blocks):
        t = cum_ref[:, m * L + L - 1 : m * L + L]
        before = before + jnp.where(m < k, t, 0.0)
        after = after + jnp.where(m > k, t, 0.0)
        own = own + jnp.where(m == k, t, 0.0)
    state = s_ref[0] + spread(jnp.exp(before), width) * s0[...]
    adj = a_ref[0] + spread(jnp.exp(after), width) * a0[...]
    state_h = state.astype(BF16)
    adj_h = adj.astype(BF16)
    b = b_ref[...]
    c = c_ref[...]
    carried = mm(c, state_h, 1, 0)
    dscaled = mm(b, adj_h, 1, 0)
    used = col_ref[:, 4 * heads : 4 * heads + 1]
    lane = lax.broadcasted_iota(jnp.int32, (L, 128), 1)
    packed = -r_ref[...]
    dqs, scs = [], []
    inflow = []
    fed = []
    for h in range(heads):
        cs = slice(h * width, (h + 1) * width)
        st = col_ref[:, h : h + 1]
        e = col_ref[:, heads + h : heads + h + 1]
        tail = col_ref[:, 2 * heads + h : 2 * heads + h + 1]
        x = x_ref[:, cs].astype(F32)
        g = g_ref[:, cs].astype(F32)
        dq = g * e
        dqs.append(dq.astype(BF16))
        u = (x * st).astype(BF16).astype(F32)
        sc = u * tail
        scs.append(sc.astype(BF16))
        ds = dscaled[:, cs]
        out = sc * ds
        local = dq * carried[:, cs] - out
        fed.append(jnp.sum(out, axis=0, keepdims=True))
        du = du_ref[:, cs].astype(F32) + ds * tail
        dx_ref[:, cs] = ((gain[h] * used) * g + du * st).astype(BF16)
        q2 = jnp.sum(local, axis=1, keepdims=True)
        dst = jnp.sum(x * du, axis=1, keepdims=True)
        packed = jnp.where(lane == h, packed + q2, packed)
        packed = jnp.where(lane == heads + h, dst, packed)
        inflow.append(jnp.sum(adj[:, cs] * state[:, cs], axis=0, keepdims=True))
    dq_all = jnp.concatenate(dqs, axis=1)
    sc_all = jnp.concatenate(scs, axis=1)
    dc_ref[...] = dc1_ref[...] + mm(dq_all, state_h, 1, 1)
    db_ref[...] = db1_ref[...] + mm(sc_all, adj_h, 1, 1)
    flow = jnp.sum(jnp.concatenate(inflow, axis=0), axis=1, keepdims=True) * jnp.exp(own)
    flow = flow + jnp.sum(jnp.concatenate(fed, axis=0), axis=1, keepdims=True)
    rows = packed.T
    at = k * L + lax.broadcasted_iota(jnp.int32, (heads, L), 1)
    live = (at < count[0]).astype(F32)
    dcum = rows[0:heads] + q_ref[...]
    ddecay_ref[...] = (running(dcum, True) + flow) * live
    dstep_ref[...] = rows[heads : 2 * heads] * live


def across(count, gain, x, g, b, c, cum, col, s, a, got, du, db1, dc1, q, r):
    heads, rows = cum.shape
    blocks = rows // L
    n = b.shape[1]
    wide = x.shape[1]
    fwd = lambda k: (k, 0)
    side = lambda k: (0, k)
    return pl.pallas_call(
        outer_kernel,
        grid=(blocks,),
        in_specs=[
            pl.BlockSpec(memory_space=pltpu.SMEM),
            pl.BlockSpec(memory_space=pltpu.SMEM),
            pl.BlockSpec((L, wide), fwd),
            pl.BlockSpec((L, wide), fwd),
            pl.BlockSpec((L, n), fwd),
            pl.BlockSpec((L, n), fwd),
            pl.BlockSpec((heads, rows), lambda k: (0, 0)),
            pl.BlockSpec((L, 128), fwd),
            pl.BlockSpec((1, n, wide), lambda k: (k, 0, 0)),
            pl.BlockSpec((1, n, wide), lambda k: (k, 0, 0)),
            pl.BlockSpec(got.shape, lambda k: (0, 0, 0, 0)),
            pl.BlockSpec((L, wide), fwd),
            pl.BlockSpec((L, n), fwd),
            pl.BlockSpec((L, n), fwd),
            pl.BlockSpec((heads, L), side),
            pl.BlockSpec((L, 128), fwd),
        ],
        out_specs=[
            pl.BlockSpec((L, wide), fwd),
            pl.BlockSpec((L, n), fwd),
            pl.BlockSpec((L, n), fwd),
            pl.BlockSpec((heads, L), side),
            pl.BlockSpec((heads, L), side),
        ],
        out_shape=[
            jax.ShapeDtypeStruct((rows, wide), BF16),
            jax.ShapeDtypeStruct((rows, n), F32),
            jax.ShapeDtypeStruct((rows, n), F32),
            jax.ShapeDtypeStruct((heads, rows), F32),
            jax.ShapeDtypeStruct((heads, rows), F32),
        ],
        scratch_shapes=[pltpu.VMEM((n, wide), F32), pltpu.VMEM((n, wide), F32)],
        compiler_params=pltpu.CompilerParams(vmem_limit_bytes=VMEM_LIMIT),
        name="across_blocks",
    )(count, gain, x, g, b, c, cum, col, s, a, got, du, db1, dc1, q, r)


def total_over_tp(first, second):
    up = [(i, (i + 1) % 4) for i in range(4)]
    down = [(i, (i + 3) % 4) for i in range(4)]
    me = lax.axis_index("tp")
    rows, n = first.shape
    one = first.reshape(4, rows // 4, n)
    two = second.reshape(4, rows // 4, n)
    pick = lambda v, k: lax.dynamic_index_in_dim(v, (me + k) % 4, 0, keepdims=False)
    send = lambda v, way: lax.ppermute(v, "tp", way)
    a1 = send(pick(one, 2), up)
    b1 = send(pick(two, 2), down)
    a2 = send(pick(one, 3), down)
    b2 = send(pick(two, 1), up)
    a3 = send(a1 + pick(one, 1), up)
    b3 = send(b1 + pick(two, 3), down)
    ra = pick(one, 0) + a2 + a3
    rb = pick(two, 0) + b2 + b3
    ga1, gb1 = send(ra, up), send(rb, down)
    ga2, gb2 = send(ra, down), send(rb, up)
    ga3, gb3 = send(ga1, up), send(gb1, down)

    def whole(own, from_below, from_above, far):
        out = jnp.zeros((4,) + own.shape, F32)
        for k, v in ((0, own), (3, from_below), (1, from_above), (2, far)):
            out = lax.dynamic_update_index_in_dim(out, v, (me + k) % 4, 0)
        return out.reshape(rows, n)

    return whole(ra, ga1, ga2, ga3), whole(rb, gb2, gb1, gb3)


def shards(x, b, c, step, decay, gain, count, g):
    devices = lax.axis_size("ctx")
    cum, col, s, a, send = local_states(count, x, g, b, c, step, decay, devices)
    got = lax.all_to_all(send, "ctx", 0, 0, tiled=True)
    du, db1, dc1, q, r = within(x, g, b, c, cum, col)
    out = scan_devices(got)
    got = lax.all_to_all(out, "ctx", 0, 0, tiled=True)
    dx, db, dc, dstep, ddecay = across(
        count, gain, x, g, b, c, cum, col, s, a, got, du, db1, dc1, q, r
    )
    db, dc = total_over_tp(db, dc)
    return dx, db, dc, dstep, ddecay


def solution(mesh):
    placed = (
        P("ctx", "tp"), P("ctx", None), P("ctx", None), P("tp", "ctx"),
        P("tp", "ctx"), P("tp"), P("ctx"), P("ctx", "tp"),
    )
    return jax.shard_map(
        shards,
        mesh=mesh,
        in_specs=placed,
        out_specs=(P("ctx", "tp"), P("ctx", None), P("ctx", None), P("tp", "ctx"), P("tp", "ctx")),
        check_vma=False,
    )
```

```python
import jax
import jax.numpy as jnp
from jax import lax
from jax.experimental import pallas as pl
from jax.experimental.pallas import tpu as pltpu
from jax.sharding import PartitionSpec as P

L = 256
F32 = jnp.float32
BF16 = jnp.bfloat16
FIRST, SECOND = 4, 2
VMEM_LIMIT = 56 * 1024 * 1024


def mm(a, b, ca, cb):
    return lax.dot_general(a, b, (((ca,), (cb,)), ((), ())), preferred_element_type=F32)


def running(rows, reverse):
    j = lax.broadcasted_iota(jnp.int32, (L, L), 0)
    i = lax.broadcasted_iota(jnp.int32, (L, L), 1)
    tri = ((j >= i) if reverse else (j <= i)).astype(F32)
    return lax.dot_general(
        rows, tri, (((1,), (0,)), ((), ())),
        precision=lax.Precision.HIGHEST, preferred_element_type=F32,
    )


def spread(v, width):
    return jnp.concatenate(
        [jnp.broadcast_to(v[h : h + 1, :], (1, width)) for h in range(v.shape[0])], axis=1
    )


def faded(ref, by):
    heads = by.shape[1]
    width = ref.shape[1] // heads
    return jnp.concatenate(
        [
            (ref[:, h * width : (h + 1) * width].astype(F32) * by[:, h : h + 1]).astype(BF16)
            for h in range(heads)
        ],
        axis=1,
    )


def states_kernel(
    count, x_ref, g_ref, b_ref, c_ref, step_ref, decay_ref,
    cum_ref, col_ref, s_ref, a_ref, send_ref, s_acc, a_acc, tot,
):
    heads = step_ref.shape[0]
    blocks = step_ref.shape[1] // L
    width = x_ref.shape[1] // heads
    k = pl.program_id(0)

    @pl.when(k == 0)
    def _():
        s_acc[...] = jnp.zeros_like(s_acc)
        a_acc[...] = jnp.zeros_like(a_acc)
        lives = []
        for n in range(blocks):
            at = n * L + lax.broadcasted_iota(jnp.int32, (heads, L), 1)
            lives.append((at < count[0]).astype(F32))
        sums = running(
            jnp.concatenate(
                [decay_ref[:, n * L : (n + 1) * L] * lives[n] for n in range(blocks)], axis=0
            ),
            False,
        )
        for n in range(blocks):
            sl = pl.ds(n * L, L)
            used = lives[n]
            st = step_ref[:, sl] * used
            cum = sums[n * heads : (n + 1) * heads]
            cum_ref[:, sl] = cum
            total = cum[:, L - 1 :]
            tot[n] = jnp.broadcast_to(total, (heads, 128))
            rows = jnp.concatenate(
                [st, jnp.exp(cum) * used, jnp.exp(total - cum) * st, cum, used,
                 jnp.zeros((128 - 5 * heads, L), F32)], axis=0
            )
            col_ref[sl, :] = rows.T

    s_ref[0] = s_acc[...].astype(BF16)
    rows = pl.ds(pl.multiple_of(k * L, L), L)
    sc = faded(x_ref, col_ref[rows, 2 * heads : 3 * heads])
    s_acc[...] = spread(jnp.exp(tot[k][:, :1]), width) * s_acc[...] + mm(
        b_ref[...].T, sc, 1, 0
    )

    back = blocks - 1 - k
    a_ref[0] = a_acc[...].astype(BF16)
    rows = pl.ds(pl.multiple_of(back * L, L), L)
    dq = faded(g_ref, col_ref[rows, heads : 2 * heads])
    a_acc[...] = spread(jnp.exp(tot[back][:, :1]), width) * a_acc[...] + mm(
        c_ref[...].T, dq, 1, 0
    )

    @pl.when(k == blocks - 1)
    def _():
        whole = tot[0]
        for n in range(1, blocks):
            whole = whole + tot[n]
        d = jnp.exp(whole)
        n_dev = send_ref.shape[0]
        each = s_acc.shape[0] // n_dev
        wide = s_acc.shape[1]
        for i in range(n_dev):
            send_ref[i, 0:each, 0:wide] = s_acc[i * each : (i + 1) * each, :]
            send_ref[i, each : 2 * each, 0:wide] = a_acc[i * each : (i + 1) * each, :]
            send_ref[i, :, wide:] = d


def local_states(count, x, g, b, c, step, decay, devices):
    heads, rows = step.shape
    blocks = rows // L
    n = b.shape[1]
    wide = x.shape[1]
    each = n // devices
    fwd = lambda k: (k, 0)
    rev = lambda k: (blocks - 1 - k, 0)
    whole = lambda k: (0, 0)
    return pl.pallas_call(
        states_kernel,
        grid=(blocks,),
        in_specs=[
            pl.BlockSpec(memory_space=pltpu.SMEM),
            pl.BlockSpec((L, wide), fwd),
            pl.BlockSpec((L, wide), rev),
            pl.BlockSpec((L, n), fwd),
            pl.BlockSpec((L, n), rev),
            pl.BlockSpec((heads, rows), whole),
            pl.BlockSpec((heads, rows), whole),
        ],
        out_specs=[
            pl.BlockSpec((heads, rows), whole),
            pl.BlockSpec((rows, 128), whole),
            pl.BlockSpec((1, n, wide), lambda k: (k, 0, 0)),
            pl.BlockSpec((1, n, wide), lambda k: (blocks - 1 - k, 0, 0)),
            pl.BlockSpec((devices, 2 * each, wide + 128), lambda k: (0, 0, 0)),
        ],
        out_shape=[
            jax.ShapeDtypeStruct((heads, rows), F32),
            jax.ShapeDtypeStruct((rows, 128), F32),
            jax.ShapeDtypeStruct((blocks, n, wide), BF16),
            jax.ShapeDtypeStruct((blocks, n, wide), BF16),
            jax.ShapeDtypeStruct((devices, 2 * each, wide + 128), F32),
        ],
        scratch_shapes=[
            pltpu.VMEM((n, wide), F32),
            pltpu.VMEM((n, wide), F32),
            pltpu.VMEM((blocks, heads, 128), F32),
        ],
        compiler_params=pltpu.CompilerParams(vmem_limit_bytes=VMEM_LIMIT),
        name="local_states",
    )(count, x, g, b, c, step, decay)


def scan_kernel(got_ref, out_ref):
    devices, both, wide = out_ref.shape
    each = both // 2
    heads = got_ref.shape[1]
    width = wide // heads

    def fade(i):
        d = got_ref[i, :, wide:]
        return jnp.concatenate(
            [jnp.broadcast_to(d[h : h + 1, :width], (each, width)) for h in range(heads)], axis=1
        )

    s = jnp.zeros((each, wide), F32)
    a = jnp.zeros((each, wide), F32)
    for i in range(devices):
        out_ref[i, 0:each, :] = s
        s = fade(i) * s + got_ref[i, 0:each, 0:wide]
        r = devices - 1 - i
        out_ref[r, each:both, :] = a
        a = fade(r) * a + got_ref[r, each:both, 0:wide]


def scan_devices(got):
    devices, both, lanes = got.shape
    return pl.pallas_call(
        scan_kernel,
        out_shape=jax.ShapeDtypeStruct((devices, both, lanes - 128), F32),
        compiler_params=pltpu.CompilerParams(vmem_limit_bytes=VMEM_LIMIT),
        name="scan_devices",
    )(got)


def inner_kernel(gain, x_ref, g_ref, b_ref, c_ref, cum_ref, col_ref,
                 *rest):
    dx_ref, db_ref, dc_ref, q_ref, r_ref = rest[-5:]
    heads = cum_ref.shape[0]
    width = x_ref.shape[1] // heads
    b = b_ref[...]
    c = c_ref[...]
    score = mm(b, c, 1, 1)
    j = lax.broadcasted_iota(jnp.int32, (L, L), 0)
    i = lax.broadcasted_iota(jnp.int32, (L, L), 1)
    keep = j <= i
    used = col_ref[:, 4 * heads : 4 * heads + 1]
    lane = lax.broadcasted_iota(jnp.int32, (L, 128), 1)
    dscore = jnp.zeros((L, L), F32)
    r_all = jnp.zeros((L, 128), F32)
    for h in range(heads):
        cs = slice(h * width, (h + 1) * width)
        live_g = g_ref[:, cs].astype(F32) * used
        dy = live_g.astype(BF16)
        x = x_ref[:, cs].astype(F32)
        st = col_ref[:, h : h + 1]
        u = (x * st).astype(BF16)
        gap = cum_ref[h : h + 1, :] - col_ref[:, 3 * heads + h : 3 * heads + h + 1]
        fade = jnp.exp(jnp.where(keep, gap, -1e30))
        w = (fade * score).astype(BF16)
        dw = mm(u, dy, 1, 1)
        dscore = dscore + dw * fade
        prod = dw * w.astype(F32)
        q_ref[h : h + 1, :] = jnp.sum(prod, axis=0, keepdims=True)
        du = mm(w, dy, 1, 0)
        dx_ref[:, cs] = (gain[h] * live_g + du * st).astype(BF16)
        r_all = jnp.where(lane == 2 * heads + h, jnp.sum(prod, axis=1, keepdims=True), r_all)
        r_all = jnp.where(lane == 3 * heads + h, jnp.sum(x * du, axis=1, keepdims=True), r_all)
    r_ref[...] = r_all
    ds = dscore.astype(BF16)
    db_ref[...] = mm(ds, c, 1, 0)
    dc_ref[...] = mm(ds.T, b, 1, 0)


def within(gain, x, g, b, c, cum, col, first, blocks, earlier):
    heads = cum.shape[0]
    n = b.shape[1]
    wide = x.shape[1]
    rows = x.shape[0]
    at = lambda k: (first + k, 0)
    return pl.pallas_call(
        inner_kernel,
        grid=(blocks,),
        in_specs=[
            pl.BlockSpec(memory_space=pltpu.SMEM),
            pl.BlockSpec((L, wide), at),
            pl.BlockSpec((L, wide), at),
            pl.BlockSpec((L, n), at),
            pl.BlockSpec((L, n), at),
            pl.BlockSpec((heads, L), lambda k: (0, first + k)),
            pl.BlockSpec((L, 128), at),
        ] + [pl.BlockSpec(memory_space=pl.ANY)] * len(earlier),
        out_specs=[
            pl.BlockSpec((L, wide), at),
            pl.BlockSpec((L, n), at),
            pl.BlockSpec((L, n), at),
            pl.BlockSpec((heads, L), lambda k: (0, first + k)),
            pl.BlockSpec((L, 128), at),
        ],
        out_shape=[
            jax.ShapeDtypeStruct((rows, wide), BF16),
            jax.ShapeDtypeStruct((rows, n), F32),
            jax.ShapeDtypeStruct((rows, n), F32),
            jax.ShapeDtypeStruct((heads, rows), F32),
            jax.ShapeDtypeStruct((rows, 128), F32),
        ],
        input_output_aliases={7 + i: i for i in range(len(earlier))},
        compiler_params=pltpu.CompilerParams(vmem_limit_bytes=VMEM_LIMIT),
        name="within_blocks",
    )(gain, x, g, b, c, cum, col, *earlier)


def basis_kernel(me, cum_ref, s_ref, a_ref, x_ref, g_ref, col_ref, got_ref, db1_ref, dc1_ref,
                 state_ref, adj_ref, flow_ref, up_ref, down_ref, mid_ref, own_ref, s0, a0):
    heads = cum_ref.shape[0]
    blocks = cum_ref.shape[1] // L
    n, wide = s0.shape
    width = wide // heads
    k = pl.program_id(0)
    each = got_ref.shape[1] // 2

    @pl.when(k == 0)
    def _():
        for i in range(got_ref.shape[0]):
            s0[i * each : (i + 1) * each, :] = got_ref[i, 0:each, :]
            a0[i * each : (i + 1) * each, :] = got_ref[i, each : 2 * each, :]

    before = jnp.zeros((heads, 1), F32)
    after = jnp.zeros((heads, 1), F32)
    own = jnp.zeros((heads, 1), F32)
    for m in range(blocks):
        t = cum_ref[:, m * L + L - 1 : m * L + L]
        before = before + jnp.where(m < k, t, 0.0)
        after = after + jnp.where(m > k, t, 0.0)
        own = own + jnp.where(m == k, t, 0.0)
    state = s_ref[0].astype(F32) + spread(jnp.exp(before), width) * s0[...]
    adj = a_ref[0].astype(F32) + spread(jnp.exp(after), width) * a0[...]
    state_h = state.astype(BF16)
    adj_h = adj.astype(BF16)
    state_ref[0] = state_h
    adj_ref[0] = adj_h
    dc = dc1_ref[...] + mm(faded(g_ref, col_ref[:, heads : 2 * heads]), state_h, 1, 1)
    db = db1_ref[...] + mm(faded(x_ref, col_ref[:, 2 * heads : 3 * heads]), adj_h, 1, 1)
    inflow = jnp.concatenate(
        [
            jnp.sum(
                adj[:, h * width : (h + 1) * width] * state[:, h * width : (h + 1) * width],
                axis=0, keepdims=True,
            )
            for h in range(heads)
        ],
        axis=0,
    )
    flow = jnp.sum(inflow, axis=1, keepdims=True) * jnp.exp(own)
    flow_ref[0] = jnp.broadcast_to(flow, (heads, 128))

    per = blocks // 4
    turn = lax.rem(lax.div(k, per) - me[0] + 4, 4)
    at = pl.ds(pl.multiple_of(lax.rem(k, per) * L, L), L)

    @pl.when(turn == 0)
    def _():
        own_ref[0, at, :] = db
        own_ref[1, at, :] = dc

    @pl.when(turn == 1)
    def _():
        mid_ref[0, at, :] = db
        up_ref[1, at, :] = dc

    @pl.when(turn == 2)
    def _():
        up_ref[0, at, :] = db
        down_ref[0, at, :] = dc

    @pl.when(turn == 3)
    def _():
        down_ref[1, at, :] = db
        mid_ref[1, at, :] = dc


def basis_grads(me, cum, s, a, x, g, col, got, db1, dc1):
    heads, rows = cum.shape
    n, wide = s.shape[1:]
    blocks = rows // L
    at = lambda k: (k, 0)
    layer = pl.BlockSpec((1, n, wide), lambda k: (k, 0, 0))
    pair = pl.BlockSpec((2, rows // 4, n), lambda k: (0, 0, 0))

    return pl.pallas_call(
        basis_kernel,
        grid=(blocks,),
        in_specs=[
            pl.BlockSpec(memory_space=pltpu.SMEM),
            pl.BlockSpec((heads, rows), lambda k: (0, 0)),
            layer,
            layer,
            pl.BlockSpec((L, wide), at),
            pl.BlockSpec((L, wide), at),
            pl.BlockSpec((L, 128), at),
            pl.BlockSpec(got.shape, lambda k: (0, 0, 0)),
            pl.BlockSpec((L, n), at),
            pl.BlockSpec((L, n), at),
        ],
        out_specs=[layer, layer, pl.BlockSpec((1, heads, 128), lambda k: (k, 0, 0)),
                   pair, pair, pair, pair],
        out_shape=[
            jax.ShapeDtypeStruct((blocks, n, wide), BF16),
            jax.ShapeDtypeStruct((blocks, n, wide), BF16),
            jax.ShapeDtypeStruct((blocks, heads, 128), F32),
        ] + [jax.ShapeDtypeStruct((2, rows // 4, n), F32)] * 4,
        scratch_shapes=[pltpu.VMEM((n, wide), F32), pltpu.VMEM((n, wide), F32)],
        compiler_params=pltpu.CompilerParams(vmem_limit_bytes=VMEM_LIMIT),
        name="basis_grads",
    )(me, cum, s, a, x, g, col, got, db1, dc1)


def row_kernel(first, count, x_ref, b_ref, c_ref, cum_ref, step_ref, col_ref, g_ref,
               state_ref, adj_ref, flow_ref, dx1_ref, q_ref, r_ref, *rest):
    dx_ref, dstep_ref, ddecay_ref = rest[-3:]
    heads = cum_ref.shape[0]
    width = x_ref.shape[1] // heads
    k = first + pl.program_id(0)
    carried = mm(c_ref[...], state_ref[0], 1, 0)
    fed = mm(b_ref[...], adj_ref[0], 1, 0)
    lane = lax.broadcasted_iota(jnp.int32, (L, 128), 1)
    packed = r_ref[...]
    for h in range(heads):
        cs = slice(h * width, (h + 1) * width)
        ts = col_ref[:, 2 * heads + h : 2 * heads + h + 1]
        ds = fed[:, cs]
        dx_ref[:, cs] = (dx1_ref[:, cs].astype(F32) + ds * ts).astype(BF16)
        a = jnp.sum(x_ref[:, cs].astype(F32) * ds, axis=1, keepdims=True)
        q = jnp.sum(g_ref[:, cs].astype(F32) * carried[:, cs], axis=1, keepdims=True)
        packed = jnp.where(lane == h, a, packed)
        packed = jnp.where(lane == heads + h, q, packed)
    rows = packed.T
    at = k * L + lax.broadcasted_iota(jnp.int32, (heads, L), 1)
    live = (at < count[0]).astype(F32)
    cum = cum_ref[...]
    more = jnp.exp(cum[:, L - 1 :] - cum) * rows[0:heads]
    mine = step_ref[...] * live * more
    flow = flow_ref[0][:, :1] + jnp.sum(mine, axis=1, keepdims=True)
    paid = jnp.exp(cum) * live * rows[heads : 2 * heads]
    dcum = q_ref[...] + paid - rows[2 * heads : 3 * heads] - mine
    ddecay_ref[...] = (running(dcum, True) + flow) * live
    dstep_ref[...] = (rows[3 * heads : 4 * heads] + more) * live


def row_grads(first, blocks, count, x, b, c, cum, step, col, g, state, adj, flow, dx1, q, r, earlier):
    heads, rows = cum.shape
    n = b.shape[1]
    wide = x.shape[1]
    at = lambda k: (first + k, 0)
    side = lambda k: (0, first + k)
    layer = pl.BlockSpec((1, n, wide), lambda k: (first + k, 0, 0))
    args = [count, x, b, c, cum, step, col, g, state, adj, flow, dx1, q, r]
    specs = [
        pl.BlockSpec(memory_space=pltpu.SMEM),
        pl.BlockSpec((L, wide), at),
        pl.BlockSpec((L, n), at),
        pl.BlockSpec((L, n), at),
        pl.BlockSpec((heads, L), side),
        pl.BlockSpec((heads, L), side),
        pl.BlockSpec((L, 128), at),
        pl.BlockSpec((L, wide), at),
        layer,
        layer,
        pl.BlockSpec((1, heads, 128), lambda k: (first + k, 0, 0)),
        pl.BlockSpec((L, wide), at),
        pl.BlockSpec((heads, L), lambda k: (0, first + k)),
        pl.BlockSpec((L, 128), at),
    ]
    alias = {}
    for i, v in enumerate(earlier):
        alias[len(args)] = i
        args.append(v)
        specs.append(pl.BlockSpec(memory_space=pl.ANY))

    def kernel(*refs):
        row_kernel(first, *refs)

    return pl.pallas_call(
        kernel,
        grid=(blocks,),
        in_specs=specs,
        out_specs=[
            pl.BlockSpec((L, wide), at),
            pl.BlockSpec((heads, L), side),
            pl.BlockSpec((heads, L), side),
        ],
        out_shape=[
            jax.ShapeDtypeStruct((rows, wide), BF16),
            jax.ShapeDtypeStruct((heads, rows), F32),
            jax.ShapeDtypeStruct((heads, rows), F32),
        ],
        input_output_aliases=alias,
        compiler_params=pltpu.CompilerParams(vmem_limit_bytes=VMEM_LIMIT),
        name="row_grads",
    )(*args)


def up(v):
    return lax.ppermute(v, "tp", [(i, (i + 1) % 4) for i in range(4)])


def down(v):
    return lax.ppermute(v, "tp", [(i, (i + 3) % 4) for i in range(4)])


def shards(x, b, c, step, decay, gain, count, g):
    devices = lax.axis_size("ctx")
    blocks = x.shape[0] // L
    me = lax.axis_index("tp")
    mine = me.astype(jnp.int32).reshape(1)
    cum, col, s, a, send = local_states(count, x, g, b, c, step, decay, devices)
    got = lax.all_to_all(send, "ctx", 0, 0, tiled=True)
    inner = within(gain, x, g, b, c, cum, col, 0, blocks // 2, ())
    got, inner = lax.optimization_barrier((got, inner))
    out = scan_devices(got)
    got = lax.all_to_all(out, "ctx", 0, 0, tiled=True)
    inner = within(gain, x, g, b, c, cum, col, blocks // 2, blocks // 2, inner)
    got, inner = lax.optimization_barrier((got, inner))
    dx1, db1, dc1, q, r = inner
    state, adj, flow, up1, down1, mid, own = basis_grads(
        mine, cum, s, a, x, g, col, got, db1, dc1
    )
    rows = lambda first, number, state, before: row_grads(
        first, number, count, x, b, c, cum, step, col, g, state, adj, flow, dx1, q, r, before
    )
    u, d = up(up1), down(down1)
    done = rows(0, FIRST, state, ())
    u, d, state, done = lax.optimization_barrier((u, d, state, done))
    p, w = up(u[0] + mid[0]), down(d[0] + mid[1])
    done = rows(FIRST, SECOND, state, done)
    p, w, state, done = lax.optimization_barrier((p, w, state, done))
    own = jnp.stack([own[0] + d[1] + p, own[1] + u[1] + w])
    below, above = up(own), down(own)
    done = rows(FIRST + SECOND, blocks - FIRST - SECOND, state, done)
    below, above, done = lax.optimization_barrier((below, above, done))
    dx, dstep, ddecay = done
    far = (up(below[0]), down(above[1]))
    db = jnp.zeros((4, b.shape[0] // 4, b.shape[1]), F32)
    dc = db
    for k, v in ((0, own), (3, below), (1, above), (2, far)):
        at = ((me + k) % 4, 0, 0)
        db = lax.dynamic_update_slice(db, v[0][None], at)
        dc = lax.dynamic_update_slice(dc, v[1][None], at)
    return dx, db.reshape(b.shape), dc.reshape(c.shape), dstep, ddecay


def solution(mesh):
    placed = (
        P("ctx", "tp"), P("ctx", None), P("ctx", None), P("tp", "ctx"),
        P("tp", "ctx"), P("tp"), P("ctx"), P("ctx", "tp"),
    )
    return jax.shard_map(
        shards,
        mesh=mesh,
        in_specs=placed,
        out_specs=(P("ctx", "tp"), P("ctx", None), P("ctx", None), P("tp", "ctx"), P("tp", "ctx")),
        check_vma=False,
    )
```

```python
import jax
import jax.numpy as jnp
from jax import lax
from jax.experimental import pallas as pl
from jax.experimental.pallas import tpu as pltpu
from jax.sharding import PartitionSpec as P

L = 256
F32 = jnp.float32
BF16 = jnp.bfloat16
PER = 2
FIRST = 5
VMEM_LIMIT = 56 * 1024 * 1024


def mm(a, b, ca, cb):
    return lax.dot_general(a, b, (((ca,), (cb,)), ((), ())), preferred_element_type=F32)


def running(rows, reverse):
    j = lax.broadcasted_iota(jnp.int32, (L, L), 0)
    i = lax.broadcasted_iota(jnp.int32, (L, L), 1)
    tri = ((j >= i) if reverse else (j <= i)).astype(F32)
    return lax.dot_general(
        rows, tri, (((1,), (0,)), ((), ())),
        precision=lax.Precision.HIGHEST, preferred_element_type=F32,
    )


def spread(v, width):
    return jnp.concatenate(
        [jnp.broadcast_to(v[h : h + 1, :], (1, width)) for h in range(v.shape[0])], axis=1
    )


def faded(ref, by):
    heads = by.shape[1]
    width = ref.shape[1] // heads
    return jnp.concatenate(
        [
            (ref[:, h * width : (h + 1) * width].astype(F32) * by[:, h : h + 1]).astype(BF16)
            for h in range(heads)
        ],
        axis=1,
    )


def states_kernel(
    count, x_ref, g_ref, b_ref, c_ref, step_ref, decay_ref,
    cum_ref, col_ref, s_ref, a_ref, send_ref, s_acc, a_acc, tot,
):
    heads = step_ref.shape[0]
    blocks = step_ref.shape[1] // L
    width = x_ref.shape[1] // heads
    k = pl.program_id(0)

    @pl.when(k == 0)
    def _():
        s_acc[...] = jnp.zeros_like(s_acc)
        a_acc[...] = jnp.zeros_like(a_acc)
        lives = []
        for n in range(blocks):
            at = n * L + lax.broadcasted_iota(jnp.int32, (heads, L), 1)
            lives.append((at < count[0]).astype(F32))
        sums = running(
            jnp.concatenate(
                [decay_ref[:, n * L : (n + 1) * L] * lives[n] for n in range(blocks)], axis=0
            ),
            False,
        )
        for n in range(blocks):
            sl = pl.ds(n * L, L)
            used = lives[n]
            st = step_ref[:, sl] * used
            cum = sums[n * heads : (n + 1) * heads]
            cum_ref[:, sl] = cum
            total = cum[:, L - 1 :]
            tot[n] = jnp.broadcast_to(total, (heads, 128))
            rows = jnp.concatenate(
                [st, jnp.exp(cum) * used, jnp.exp(total - cum) * st, cum, used,
                 jnp.zeros((128 - 5 * heads, L), F32)], axis=0
            )
            col_ref[sl, :] = rows.T

    for j in range(PER):
        n = k * PER + j
        s_ref[j] = s_acc[...].astype(BF16)
        rows = pl.ds(pl.multiple_of(n * L, L), L)
        at = slice(j * L, (j + 1) * L)
        sc = faded(x_ref.at[at, :], col_ref[rows, 2 * heads : 3 * heads])
        s_acc[...] = spread(jnp.exp(tot[n][:, :1]), width) * s_acc[...] + mm(
            b_ref[at, :].T, sc, 1, 0
        )

        m = PER - 1 - j
        n = blocks - 1 - n
        a_ref[m] = a_acc[...].astype(BF16)
        rows = pl.ds(pl.multiple_of(n * L, L), L)
        at = slice(m * L, (m + 1) * L)
        dq = faded(g_ref.at[at, :], col_ref[rows, heads : 2 * heads])
        a_acc[...] = spread(jnp.exp(tot[n][:, :1]), width) * a_acc[...] + mm(
            c_ref[at, :].T, dq, 1, 0
        )

    @pl.when(k == blocks // PER - 1)
    def _():
        whole = tot[0]
        for n in range(1, blocks):
            whole = whole + tot[n]
        d = jnp.exp(whole)
        n_dev = send_ref.shape[0]
        each = s_acc.shape[0] // n_dev
        wide = s_acc.shape[1]
        for i in range(n_dev):
            send_ref[i, 0:each, 0:wide] = s_acc[i * each : (i + 1) * each, :]
            send_ref[i, each : 2 * each, 0:wide] = a_acc[i * each : (i + 1) * each, :]
            send_ref[i, :, wide:] = d


def local_states(count, x, g, b, c, step, decay, devices):
    heads, rows = step.shape
    blocks = rows // L
    n = b.shape[1]
    wide = x.shape[1]
    each = n // devices
    fwd = lambda k: (k, 0)
    last = blocks // PER - 1
    rev = lambda k: (last - k, 0)
    whole = lambda k: (0, 0)
    return pl.pallas_call(
        states_kernel,
        grid=(blocks // PER,),
        in_specs=[
            pl.BlockSpec(memory_space=pltpu.SMEM),
            pl.BlockSpec((PER * L, wide), fwd),
            pl.BlockSpec((PER * L, wide), rev),
            pl.BlockSpec((PER * L, n), fwd),
            pl.BlockSpec((PER * L, n), rev),
            pl.BlockSpec((heads, rows), whole),
            pl.BlockSpec((heads, rows), whole),
        ],
        out_specs=[
            pl.BlockSpec((heads, rows), whole),
            pl.BlockSpec((rows, 128), whole),
            pl.BlockSpec((PER, n, wide), lambda k: (k, 0, 0)),
            pl.BlockSpec((PER, n, wide), lambda k: (last - k, 0, 0)),
            pl.BlockSpec((devices, 2 * each, wide + 128), lambda k: (0, 0, 0)),
        ],
        out_shape=[
            jax.ShapeDtypeStruct((heads, rows), F32),
            jax.ShapeDtypeStruct((rows, 128), F32),
            jax.ShapeDtypeStruct((blocks, n, wide), BF16),
            jax.ShapeDtypeStruct((blocks, n, wide), BF16),
            jax.ShapeDtypeStruct((devices, 2 * each, wide + 128), F32),
        ],
        scratch_shapes=[
            pltpu.VMEM((n, wide), F32),
            pltpu.VMEM((n, wide), F32),
            pltpu.VMEM((blocks, heads, 128), F32),
        ],
        compiler_params=pltpu.CompilerParams(vmem_limit_bytes=VMEM_LIMIT),
        name="local_states",
    )(count, x, g, b, c, step, decay)


def scan_kernel(got_ref, out_ref):
    devices, both, wide = out_ref.shape
    each = both // 2
    heads = got_ref.shape[1]
    width = wide // heads

    def fade(i):
        d = got_ref[i, :, wide:]
        return jnp.concatenate(
            [jnp.broadcast_to(d[h : h + 1, :width], (each, width)) for h in range(heads)], axis=1
        )

    s = jnp.zeros((each, wide), F32)
    a = jnp.zeros((each, wide), F32)
    for i in range(devices):
        out_ref[i, 0:each, :] = s
        s = fade(i) * s + got_ref[i, 0:each, 0:wide]
        r = devices - 1 - i
        out_ref[r, each:both, :] = a
        a = fade(r) * a + got_ref[r, each:both, 0:wide]


def scan_devices(got):
    devices, both, lanes = got.shape
    return pl.pallas_call(
        scan_kernel,
        out_shape=jax.ShapeDtypeStruct((devices, both, lanes - 128), F32),
        compiler_params=pltpu.CompilerParams(vmem_limit_bytes=VMEM_LIMIT),
        name="scan_devices",
    )(got)


def inner_kernel(gain, x_ref, g_ref, b_ref, c_ref, cum_ref, col_ref, s_ref, a_ref,
                 *rest):
    dx_ref, db_ref, dc_ref, q_ref, r_ref = rest[-5:]
    heads = cum_ref.shape[0]
    width = x_ref.shape[1] // heads
    b = b_ref[...]
    c = c_ref[...]
    score = mm(b, c, 1, 1)
    j = lax.broadcasted_iota(jnp.int32, (L, L), 0)
    i = lax.broadcasted_iota(jnp.int32, (L, L), 1)
    keep = j <= i
    used = col_ref[:, 4 * heads : 4 * heads + 1]
    lane = lax.broadcasted_iota(jnp.int32, (L, 128), 1)
    state = s_ref[0]
    adj = a_ref[0]
    dscore = jnp.zeros((L, L), F32)
    r_all = jnp.zeros((L, 128), F32)
    for h in range(heads):
        cs = slice(h * width, (h + 1) * width)
        live_g = g_ref[:, cs].astype(F32) * used
        dy = live_g.astype(BF16)
        x = x_ref[:, cs].astype(F32)
        st = col_ref[:, h : h + 1]
        u = (x * st).astype(BF16)
        gap = cum_ref[h : h + 1, :] - col_ref[:, 3 * heads + h : 3 * heads + h + 1]
        fade = jnp.exp(jnp.where(keep, gap, -1e30))
        w = (fade * score).astype(BF16)
        dw = mm(u, dy, 1, 1)
        dscore = dscore + dw * fade
        prod = dw * w.astype(F32)
        q_ref[h : h + 1, :] = jnp.sum(prod, axis=0, keepdims=True)
        du = mm(w, dy, 1, 0)
        dx_ref[:, cs] = (gain[h] * live_g + du * st).astype(BF16)
        r_all = jnp.where(lane == 2 * heads + h, jnp.sum(prod, axis=1, keepdims=True), r_all)
        r_all = jnp.where(lane == 3 * heads + h, jnp.sum(x * du, axis=1, keepdims=True), r_all)
    r_ref[...] = r_all
    dscore = dscore.astype(BF16)
    sc = faded(x_ref, col_ref[:, 2 * heads : 3 * heads])
    dq = faded(g_ref, col_ref[:, heads : 2 * heads])
    db_ref[...] = mm(dscore, c, 1, 0) + mm(sc, adj, 1, 1)
    dc_ref[...] = mm(dscore.T, b, 1, 0) + mm(dq, state, 1, 1)


def within(gain, x, g, b, c, cum, col, s, a, first, blocks, earlier):
    heads = cum.shape[0]
    n = b.shape[1]
    wide = x.shape[1]
    rows = x.shape[0]
    at = lambda k: (first + k, 0)
    return pl.pallas_call(
        inner_kernel,
        grid=(blocks,),
        in_specs=[
            pl.BlockSpec(memory_space=pltpu.SMEM),
            pl.BlockSpec((L, wide), at),
            pl.BlockSpec((L, wide), at),
            pl.BlockSpec((L, n), at),
            pl.BlockSpec((L, n), at),
            pl.BlockSpec((heads, L), lambda k: (0, first + k)),
            pl.BlockSpec((L, 128), at),
            pl.BlockSpec((1, n, wide), lambda k: (first + k, 0, 0)),
            pl.BlockSpec((1, n, wide), lambda k: (first + k, 0, 0)),
        ] + [pl.BlockSpec(memory_space=pl.ANY)] * len(earlier),
        out_specs=[
            pl.BlockSpec((L, wide), at),
            pl.BlockSpec((L, n), at),
            pl.BlockSpec((L, n), at),
            pl.BlockSpec((heads, L), lambda k: (0, first + k)),
            pl.BlockSpec((L, 128), at),
        ],
        out_shape=[
            jax.ShapeDtypeStruct((rows, wide), BF16),
            jax.ShapeDtypeStruct((rows, n), F32),
            jax.ShapeDtypeStruct((rows, n), F32),
            jax.ShapeDtypeStruct((heads, rows), F32),
            jax.ShapeDtypeStruct((rows, 128), F32),
        ],
        input_output_aliases={9 + i: i for i in range(len(earlier))},
        compiler_params=pltpu.CompilerParams(vmem_limit_bytes=VMEM_LIMIT),
        name="within_blocks",
    )(gain, x, g, b, c, cum, col, s, a, *earlier)


def unpack(got_ref, s0, a0):
    each = got_ref.shape[1] // 2
    for i in range(got_ref.shape[0]):
        s0[i * each : (i + 1) * each, :] = got_ref[i, 0:each, :]
        a0[i * each : (i + 1) * each, :] = got_ref[i, each : 2 * each, :]


def totals(cum_ref, k):
    heads = cum_ref.shape[0]
    before = jnp.zeros((heads, 1), F32)
    after = jnp.zeros((heads, 1), F32)
    own = jnp.zeros((heads, 1), F32)
    for m in range(cum_ref.shape[1] // L):
        t = cum_ref[:, m * L + L - 1 : m * L + L]
        before = before + jnp.where(m < k, t, 0.0)
        after = after + jnp.where(m > k, t, 0.0)
        own = own + jnp.where(m == k, t, 0.0)
    return before, after, own


def basis_kernel(me, cum_ref, x_ref, g_ref, col_ref, got_ref, db1_ref, dc1_ref,
                 up_ref, down_ref, mid_ref, own_ref, s0, a0):
    heads = cum_ref.shape[0]
    blocks = cum_ref.shape[1] // L
    width = s0.shape[1] // heads
    k = pl.program_id(0)

    @pl.when(k == 0)
    def _():
        unpack(got_ref, s0, a0)

    per = blocks // 4
    dbs, dcs = [], []
    for j in range(per):
        at = slice(j * L, (j + 1) * L)
        before, after, _ = totals(cum_ref, k * per + j)
        state = (spread(jnp.exp(before), width) * s0[...]).astype(BF16)
        adj = (spread(jnp.exp(after), width) * a0[...]).astype(BF16)
        e = col_ref[at, heads : 2 * heads]
        ts = col_ref[at, 2 * heads : 3 * heads]
        dcs.append(dc1_ref[at, :] + mm(faded(g_ref.at[at, :], e), state, 1, 1))
        dbs.append(db1_ref[at, :] + mm(faded(x_ref.at[at, :], ts), adj, 1, 1))
    db = jnp.concatenate(dbs, axis=0)
    dc = jnp.concatenate(dcs, axis=0)
    turn = lax.rem(k - me[0] + 4, 4)

    @pl.when(turn == 0)
    def _():
        own_ref[0] = db
        own_ref[1] = dc

    @pl.when(turn == 1)
    def _():
        mid_ref[0] = db
        up_ref[1] = dc

    @pl.when(turn == 2)
    def _():
        up_ref[0] = db
        down_ref[0] = dc

    @pl.when(turn == 3)
    def _():
        down_ref[1] = db
        mid_ref[1] = dc


def basis_grads(me, cum, x, g, col, got, db1, dc1):
    heads, rows = cum.shape
    n = db1.shape[1]
    wide = x.shape[1]
    part = rows // 4
    at = lambda k: (k, 0)
    pair = pl.BlockSpec((2, rows // 4, n), lambda k: (0, 0, 0))

    return pl.pallas_call(
        basis_kernel,
        grid=(4,),
        in_specs=[
            pl.BlockSpec(memory_space=pltpu.SMEM),
            pl.BlockSpec((heads, rows), lambda k: (0, 0)),
            pl.BlockSpec((part, wide), at),
            pl.BlockSpec((part, wide), at),
            pl.BlockSpec((part, 128), at),
            pl.BlockSpec(got.shape, lambda k: (0, 0, 0)),
            pl.BlockSpec((part, n), at),
            pl.BlockSpec((part, n), at),
        ],
        out_specs=[pair, pair, pair, pair],
        out_shape=[jax.ShapeDtypeStruct((2, rows // 4, n), F32)] * 4,
        scratch_shapes=[pltpu.VMEM((n, wide), F32), pltpu.VMEM((n, wide), F32)],
        compiler_params=pltpu.CompilerParams(vmem_limit_bytes=VMEM_LIMIT),
        name="basis_grads",
    )(me, cum, x, g, col, got, db1, dc1)


def row_kernel(first, count, x_ref, b_ref, c_ref, cum_ref, step_ref, col_ref, g_ref,
               s_ref, a_ref, got_ref, dx1_ref, q_ref, r_ref, *rest):
    dx_ref, dstep_ref, ddecay_ref, s0, a0 = rest[-5:]
    heads = cum_ref.shape[0]
    width = x_ref.shape[1] // heads
    k = first + pl.program_id(0)

    @pl.when(pl.program_id(0) == 0)
    def _():
        unpack(got_ref, s0, a0)

    before, after, own = totals(cum_ref, k)
    state = s_ref[0].astype(F32) + spread(jnp.exp(before), width) * s0[...]
    adj = a_ref[0].astype(F32) + spread(jnp.exp(after), width) * a0[...]
    carried = mm(c_ref[...], state.astype(BF16), 1, 0)
    fed = mm(b_ref[...], adj.astype(BF16), 1, 0)
    inflow = []
    lane = lax.broadcasted_iota(jnp.int32, (L, 128), 1)
    packed = r_ref[...]
    for h in range(heads):
        cs = slice(h * width, (h + 1) * width)
        ts = col_ref[:, 2 * heads + h : 2 * heads + h + 1]
        ds = fed[:, cs]
        dx_ref[:, cs] = (dx1_ref[:, cs].astype(F32) + ds * ts).astype(BF16)
        a = jnp.sum(x_ref[:, cs].astype(F32) * ds, axis=1, keepdims=True)
        q = jnp.sum(g_ref[:, cs].astype(F32) * carried[:, cs], axis=1, keepdims=True)
        packed = jnp.where(lane == h, a, packed)
        packed = jnp.where(lane == heads + h, q, packed)
        inflow.append(jnp.sum(adj[:, cs] * state[:, cs], axis=0, keepdims=True))
    rows = packed.T
    at = k * L + lax.broadcasted_iota(jnp.int32, (heads, L), 1)
    live = (at < count[0]).astype(F32)
    cum = cum_ref[:, pl.ds(pl.multiple_of(k * L, L), L)]
    more = jnp.exp(own - cum) * rows[0:heads]
    mine = step_ref[...] * live * more
    flow = jnp.sum(jnp.concatenate(inflow, axis=0), axis=1, keepdims=True) * jnp.exp(own)
    flow = flow + jnp.sum(mine, axis=1, keepdims=True)
    paid = jnp.exp(cum) * live * rows[heads : 2 * heads]
    dcum = q_ref[...] + paid - rows[2 * heads : 3 * heads] - mine
    ddecay_ref[...] = (running(dcum, True) + flow) * live
    dstep_ref[...] = (rows[3 * heads : 4 * heads] + more) * live


def row_grads(first, blocks, count, x, b, c, cum, step, col, g, s, a, got, dx1, q, r, earlier):
    heads, rows = cum.shape
    n = b.shape[1]
    wide = x.shape[1]
    at = lambda k: (first + k, 0)
    side = lambda k: (0, first + k)
    layer = pl.BlockSpec((1, n, wide), lambda k: (first + k, 0, 0))
    args = [count, x, b, c, cum, step, col, g, s, a, got, dx1, q, r]
    specs = [
        pl.BlockSpec(memory_space=pltpu.SMEM),
        pl.BlockSpec((L, wide), at),
        pl.BlockSpec((L, n), at),
        pl.BlockSpec((L, n), at),
        pl.BlockSpec((heads, rows), lambda k: (0, 0)),
        pl.BlockSpec((heads, L), side),
        pl.BlockSpec((L, 128), at),
        pl.BlockSpec((L, wide), at),
        layer,
        layer,
        pl.BlockSpec(got.shape, lambda k: (0, 0, 0)),
        pl.BlockSpec((L, wide), at),
        pl.BlockSpec((heads, L), lambda k: (0, first + k)),
        pl.BlockSpec((L, 128), at),
    ]
    alias = {}
    for i, v in enumerate(earlier):
        alias[len(args)] = i
        args.append(v)
        specs.append(pl.BlockSpec(memory_space=pl.ANY))

    def kernel(*refs):
        row_kernel(first, *refs)

    return pl.pallas_call(
        kernel,
        grid=(blocks,),
        in_specs=specs,
        out_specs=[
            pl.BlockSpec((L, wide), at),
            pl.BlockSpec((heads, L), side),
            pl.BlockSpec((heads, L), side),
        ],
        out_shape=[
            jax.ShapeDtypeStruct((rows, wide), BF16),
            jax.ShapeDtypeStruct((heads, rows), F32),
            jax.ShapeDtypeStruct((heads, rows), F32),
        ],
        scratch_shapes=[pltpu.VMEM((n, wide), F32), pltpu.VMEM((n, wide), F32)],
        input_output_aliases=alias,
        compiler_params=pltpu.CompilerParams(vmem_limit_bytes=VMEM_LIMIT),
        name="row_grads",
    )(*args)


def up(v):
    return lax.ppermute(v, "tp", [(i, (i + 1) % 4) for i in range(4)])


def down(v):
    return lax.ppermute(v, "tp", [(i, (i + 3) % 4) for i in range(4)])


def shards(x, b, c, step, decay, gain, count, g):
    devices = lax.axis_size("ctx")
    blocks = x.shape[0] // L
    me = lax.axis_index("tp")
    mine = me.astype(jnp.int32).reshape(1)
    cum, col, s, a, send = local_states(count, x, g, b, c, step, decay, devices)
    got = lax.all_to_all(send, "ctx", 0, 0, tiled=True)
    inner = within(gain, x, g, b, c, cum, col, s, a, 0, blocks // 2, ())
    got, inner = lax.optimization_barrier((got, inner))
    out = scan_devices(got)
    got = lax.all_to_all(out, "ctx", 0, 0, tiled=True)
    inner = within(gain, x, g, b, c, cum, col, s, a, blocks // 2, blocks // 2, inner)
    got, inner = lax.optimization_barrier((got, inner))
    dx1, db1, dc1, q, r = inner
    up1, down1, mid, own = basis_grads(mine, cum, x, g, col, got, db1, dc1)
    rows = lambda first, number, state, before: row_grads(
        first, number, count, x, b, c, cum, step, col, g, state, a, got, dx1, q, r, before
    )
    u, d = up(up1), down(down1)
    done = rows(0, FIRST, s, ())
    u, d, state, done = lax.optimization_barrier((u, d, s, done))
    p, w = up(u[0] + mid[0]), down(d[0] + mid[1])
    own = jnp.stack([own[0] + d[1] + p, own[1] + u[1] + w])
    own, state, done = lax.optimization_barrier((own, state, done))
    below, above = up(own), down(own)
    done = rows(FIRST, blocks - FIRST, state, done)
    below, above, done = lax.optimization_barrier((below, above, done))
    dx, dstep, ddecay = done
    far = (up(below[0]), down(above[1]))
    db = jnp.zeros((4, b.shape[0] // 4, b.shape[1]), F32)
    dc = db
    for k, v in ((0, own), (3, below), (1, above), (2, far)):
        at = ((me + k) % 4, 0, 0)
        db = lax.dynamic_update_slice(db, v[0][None], at)
        dc = lax.dynamic_update_slice(dc, v[1][None], at)
    return dx, db.reshape(b.shape), dc.reshape(c.shape), dstep, ddecay


def solution(mesh):
    placed = (
        P("ctx", "tp"), P("ctx", None), P("ctx", None), P("tp", "ctx"),
        P("tp", "ctx"), P("tp"), P("ctx"), P("ctx", "tp"),
    )
    return jax.shard_map(
        shards,
        mesh=mesh,
        in_specs=placed,
        out_specs=(P("ctx", "tp"), P("ctx", None), P("ctx", None), P("tp", "ctx"), P("tp", "ctx")),
        check_vma=False,
    )
```

```python
import jax
import jax.numpy as jnp
from jax import lax
from jax.experimental import pallas as pl
from jax.experimental.pallas import tpu as pltpu
from jax.sharding import PartitionSpec as P

L = 256
F32 = jnp.float32
BF16 = jnp.bfloat16
PER = 2
FIRST = 5
VMEM_LIMIT = 56 * 1024 * 1024


def mm(a, b, ca, cb):
    return lax.dot_general(a, b, (((ca,), (cb,)), ((), ())), preferred_element_type=F32)


def running(rows, reverse):
    j = lax.broadcasted_iota(jnp.int32, (L, L), 0)
    i = lax.broadcasted_iota(jnp.int32, (L, L), 1)
    tri = ((j >= i) if reverse else (j <= i)).astype(F32)
    return lax.dot_general(
        rows, tri, (((1,), (0,)), ((), ())),
        precision=lax.Precision.HIGHEST, preferred_element_type=F32,
    )


def spread(v, width):
    return jnp.concatenate(
        [jnp.broadcast_to(v[h : h + 1, :], (1, width)) for h in range(v.shape[0])], axis=1
    )


def faded(ref, by):
    heads = by.shape[1]
    width = ref.shape[1] // heads
    return jnp.concatenate(
        [
            (ref[:, h * width : (h + 1) * width].astype(F32) * by[:, h : h + 1]).astype(BF16)
            for h in range(heads)
        ],
        axis=1,
    )


def states_kernel(
    count, x_ref, g_ref, b_ref, c_ref, step_ref, decay_ref,
    cum_ref, col_ref, s_ref, a_ref, send_ref, s_acc, a_acc, tot,
):
    heads = step_ref.shape[0]
    blocks = step_ref.shape[1] // L
    width = x_ref.shape[1] // heads
    k = pl.program_id(0)

    @pl.when(k == 0)
    def _():
        s_acc[...] = jnp.zeros_like(s_acc)
        a_acc[...] = jnp.zeros_like(a_acc)
        lives = []
        for n in range(blocks):
            at = n * L + lax.broadcasted_iota(jnp.int32, (heads, L), 1)
            lives.append((at < count[0]).astype(F32))
        sums = running(
            jnp.concatenate(
                [decay_ref[:, n * L : (n + 1) * L] * lives[n] for n in range(blocks)], axis=0
            ),
            False,
        )
        for n in range(blocks):
            sl = pl.ds(n * L, L)
            used = lives[n]
            st = step_ref[:, sl] * used
            cum = sums[n * heads : (n + 1) * heads]
            cum_ref[:, sl] = cum
            total = cum[:, L - 1 :]
            tot[n] = jnp.broadcast_to(total, (heads, 128))
            rows = jnp.concatenate(
                [st, jnp.exp(cum) * used, jnp.exp(total - cum) * st, cum, used,
                 jnp.zeros((128 - 5 * heads, L), F32)], axis=0
            )
            col_ref[sl, :] = rows.T

    for j in range(PER):
        n = k * PER + j
        s_ref[j] = s_acc[...].astype(BF16)
        rows = pl.ds(pl.multiple_of(n * L, L), L)
        at = slice(j * L, (j + 1) * L)
        sc = faded(x_ref.at[at, :], col_ref[rows, 2 * heads : 3 * heads])
        s_acc[...] = spread(jnp.exp(tot[n][:, :1]), width) * s_acc[...] + mm(
            b_ref[at, :].T, sc, 1, 0
        )

        m = PER - 1 - j
        n = blocks - 1 - n
        a_ref[m] = a_acc[...].astype(BF16)
        rows = pl.ds(pl.multiple_of(n * L, L), L)
        at = slice(m * L, (m + 1) * L)
        dq = faded(g_ref.at[at, :], col_ref[rows, heads : 2 * heads])
        a_acc[...] = spread(jnp.exp(tot[n][:, :1]), width) * a_acc[...] + mm(
            c_ref[at, :].T, dq, 1, 0
        )

    @pl.when(k == blocks // PER - 1)
    def _():
        whole = tot[0]
        for n in range(1, blocks):
            whole = whole + tot[n]
        d = jnp.exp(whole)
        n_dev = send_ref.shape[0]
        each = s_acc.shape[0] // n_dev
        wide = s_acc.shape[1]
        for i in range(n_dev):
            send_ref[i, 0:each, 0:wide] = s_acc[i * each : (i + 1) * each, :]
            send_ref[i, each : 2 * each, 0:wide] = a_acc[i * each : (i + 1) * each, :]
            send_ref[i, :, wide:] = d


def local_states(count, x, g, b, c, step, decay, devices):
    heads, rows = step.shape
    blocks = rows // L
    n = b.shape[1]
    wide = x.shape[1]
    each = n // devices
    fwd = lambda k: (k, 0)
    last = blocks // PER - 1
    rev = lambda k: (last - k, 0)
    whole = lambda k: (0, 0)
    return pl.pallas_call(
        states_kernel,
        grid=(blocks // PER,),
        in_specs=[
            pl.BlockSpec(memory_space=pltpu.SMEM),
            pl.BlockSpec((PER * L, wide), fwd),
            pl.BlockSpec((PER * L, wide), rev),
            pl.BlockSpec((PER * L, n), fwd),
            pl.BlockSpec((PER * L, n), rev),
            pl.BlockSpec((heads, rows), whole),
            pl.BlockSpec((heads, rows), whole),
        ],
        out_specs=[
            pl.BlockSpec((heads, rows), whole),
            pl.BlockSpec((rows, 128), whole),
            pl.BlockSpec((PER, n, wide), lambda k: (k, 0, 0)),
            pl.BlockSpec((PER, n, wide), lambda k: (last - k, 0, 0)),
            pl.BlockSpec((devices, 2 * each, wide + 128), lambda k: (0, 0, 0)),
        ],
        out_shape=[
            jax.ShapeDtypeStruct((heads, rows), F32),
            jax.ShapeDtypeStruct((rows, 128), F32),
            jax.ShapeDtypeStruct((blocks, n, wide), BF16),
            jax.ShapeDtypeStruct((blocks, n, wide), BF16),
            jax.ShapeDtypeStruct((devices, 2 * each, wide + 128), F32),
        ],
        scratch_shapes=[
            pltpu.VMEM((n, wide), F32),
            pltpu.VMEM((n, wide), F32),
            pltpu.VMEM((blocks, heads, 128), F32),
        ],
        compiler_params=pltpu.CompilerParams(vmem_limit_bytes=VMEM_LIMIT),
        name="local_states",
    )(count, x, g, b, c, step, decay)


def scan_kernel(got_ref, out_ref):
    devices, both, wide = out_ref.shape
    each = both // 2
    heads = got_ref.shape[1]
    width = wide // heads

    def fade(i):
        d = got_ref[i, :, wide:]
        return jnp.concatenate(
            [jnp.broadcast_to(d[h : h + 1, :width], (each, width)) for h in range(heads)], axis=1
        )

    s = jnp.zeros((each, wide), F32)
    a = jnp.zeros((each, wide), F32)
    for i in range(devices):
        out_ref[i, 0:each, :] = s
        s = fade(i) * s + got_ref[i, 0:each, 0:wide]
        r = devices - 1 - i
        out_ref[r, each:both, :] = a
        a = fade(r) * a + got_ref[r, each:both, 0:wide]


def scan_devices(got):
    devices, both, lanes = got.shape
    return pl.pallas_call(
        scan_kernel,
        out_shape=jax.ShapeDtypeStruct((devices, both, lanes - 128), F32),
        compiler_params=pltpu.CompilerParams(vmem_limit_bytes=8 * 1024 * 1024),
        name="scan_devices",
    )(got)


def inner_kernel(gain, x_ref, g_ref, b_ref, c_ref, cum_ref, col_ref, s_ref, a_ref,
                 *rest):
    dx_ref, db_ref, dc_ref, q_ref, r_ref = rest[-5:]
    heads = cum_ref.shape[0]
    width = x_ref.shape[1] // heads
    b = b_ref[...]
    c = c_ref[...]
    score = mm(b, c, 1, 1)
    j = lax.broadcasted_iota(jnp.int32, (L, L), 0)
    i = lax.broadcasted_iota(jnp.int32, (L, L), 1)
    keep = j <= i
    used = col_ref[:, 4 * heads : 4 * heads + 1]
    lane = lax.broadcasted_iota(jnp.int32, (L, 128), 1)
    state = s_ref[0]
    adj = a_ref[0]
    dscore = jnp.zeros((L, L), F32)
    r_all = jnp.zeros((L, 128), F32)
    for h in range(heads):
        cs = slice(h * width, (h + 1) * width)
        live_g = g_ref[:, cs].astype(F32) * used
        dy = live_g.astype(BF16)
        x = x_ref[:, cs].astype(F32)
        st = col_ref[:, h : h + 1]
        u = (x * st).astype(BF16)
        gap = cum_ref[h : h + 1, :] - col_ref[:, 3 * heads + h : 3 * heads + h + 1]
        fade = jnp.exp(jnp.where(keep, gap, -1e30))
        w = (fade * score).astype(BF16)
        dw = mm(u, dy, 1, 1)
        dscore = dscore + dw * fade
        prod = dw * w.astype(F32)
        q_ref[h : h + 1, :] = jnp.sum(prod, axis=0, keepdims=True)
        du = mm(w, dy, 1, 0)
        dx_ref[:, cs] = (gain[h] * live_g + du * st).astype(BF16)
        r_all = jnp.where(lane == 2 * heads + h, jnp.sum(prod, axis=1, keepdims=True), r_all)
        r_all = jnp.where(lane == 3 * heads + h, jnp.sum(x * du, axis=1, keepdims=True), r_all)
    r_ref[...] = r_all
    dscore = dscore.astype(BF16)
    sc = faded(x_ref, col_ref[:, 2 * heads : 3 * heads])
    dq = faded(g_ref, col_ref[:, heads : 2 * heads])
    db_ref[...] = mm(dscore, c, 1, 0) + mm(sc, adj, 1, 1)
    dc_ref[...] = mm(dscore.T, b, 1, 0) + mm(dq, state, 1, 1)


def within(gain, x, g, b, c, cum, col, s, a, first, blocks, earlier):
    heads = cum.shape[0]
    n = b.shape[1]
    wide = x.shape[1]
    rows = x.shape[0]
    at = lambda k: (first + k, 0)
    return pl.pallas_call(
        inner_kernel,
        grid=(blocks,),
        in_specs=[
            pl.BlockSpec(memory_space=pltpu.SMEM),
            pl.BlockSpec((L, wide), at),
            pl.BlockSpec((L, wide), at),
            pl.BlockSpec((L, n), at),
            pl.BlockSpec((L, n), at),
            pl.BlockSpec((heads, L), lambda k: (0, first + k)),
            pl.BlockSpec((L, 128), at),
            pl.BlockSpec((1, n, wide), lambda k: (first + k, 0, 0)),
            pl.BlockSpec((1, n, wide), lambda k: (first + k, 0, 0)),
        ] + [pl.BlockSpec(memory_space=pl.ANY)] * len(earlier),
        out_specs=[
            pl.BlockSpec((L, wide), at),
            pl.BlockSpec((L, n), at),
            pl.BlockSpec((L, n), at),
            pl.BlockSpec((heads, L), lambda k: (0, first + k)),
            pl.BlockSpec((L, 128), at),
        ],
        out_shape=[
            jax.ShapeDtypeStruct((rows, wide), BF16),
            jax.ShapeDtypeStruct((rows, n), F32),
            jax.ShapeDtypeStruct((rows, n), F32),
            jax.ShapeDtypeStruct((heads, rows), F32),
            jax.ShapeDtypeStruct((rows, 128), F32),
        ],
        input_output_aliases={9 + i: i for i in range(len(earlier))},
        compiler_params=pltpu.CompilerParams(vmem_limit_bytes=VMEM_LIMIT),
        name="within_blocks",
    )(gain, x, g, b, c, cum, col, s, a, *earlier)


def unpack(got_ref, s0, a0):
    each = got_ref.shape[1] // 2
    for i in range(got_ref.shape[0]):
        s0[i * each : (i + 1) * each, :] = got_ref[i, 0:each, :]
        a0[i * each : (i + 1) * each, :] = got_ref[i, each : 2 * each, :]


def totals(cum_ref, k):
    heads = cum_ref.shape[0]
    before = jnp.zeros((heads, 1), F32)
    after = jnp.zeros((heads, 1), F32)
    own = jnp.zeros((heads, 1), F32)
    for m in range(cum_ref.shape[1] // L):
        t = cum_ref[:, m * L + L - 1 : m * L + L]
        before = before + jnp.where(m < k, t, 0.0)
        after = after + jnp.where(m > k, t, 0.0)
        own = own + jnp.where(m == k, t, 0.0)
    return before, after, own


def basis_kernel(me, cum_ref, x_ref, g_ref, col_ref, got_ref, db1_ref, dc1_ref,
                 up_ref, down_ref, mid_ref, own_ref, s0, a0):
    heads = cum_ref.shape[0]
    blocks = cum_ref.shape[1] // L
    width = s0.shape[1] // heads
    k = pl.program_id(0)

    @pl.when(k == 0)
    def _():
        unpack(got_ref, s0, a0)

    per = blocks // 4
    dbs, dcs = [], []
    for j in range(per):
        at = slice(j * L, (j + 1) * L)
        before, after, _ = totals(cum_ref, k * per + j)
        state = (spread(jnp.exp(before), width) * s0[...]).astype(BF16)
        adj = (spread(jnp.exp(after), width) * a0[...]).astype(BF16)
        e = col_ref[at, heads : 2 * heads]
        ts = col_ref[at, 2 * heads : 3 * heads]
        dcs.append(dc1_ref[at, :] + mm(faded(g_ref.at[at, :], e), state, 1, 1))
        dbs.append(db1_ref[at, :] + mm(faded(x_ref.at[at, :], ts), adj, 1, 1))
    db = jnp.concatenate(dbs, axis=0)
    dc = jnp.concatenate(dcs, axis=0)
    turn = lax.rem(k - me[0] + 4, 4)

    @pl.when(turn == 0)
    def _():
        own_ref[0] = db
        own_ref[1] = dc

    @pl.when(turn == 1)
    def _():
        mid_ref[0] = db
        up_ref[1] = dc

    @pl.when(turn == 2)
    def _():
        up_ref[0] = db
        down_ref[0] = dc

    @pl.when(turn == 3)
    def _():
        down_ref[1] = db
        mid_ref[1] = dc


def basis_grads(me, cum, x, g, col, got, db1, dc1):
    heads, rows = cum.shape
    n = db1.shape[1]
    wide = x.shape[1]
    part = rows // 4
    at = lambda k: (k, 0)
    pair = pl.BlockSpec((2, rows // 4, n), lambda k: (0, 0, 0))

    return pl.pallas_call(
        basis_kernel,
        grid=(4,),
        in_specs=[
            pl.BlockSpec(memory_space=pltpu.SMEM),
            pl.BlockSpec((heads, rows), lambda k: (0, 0)),
            pl.BlockSpec((part, wide), at),
            pl.BlockSpec((part, wide), at),
            pl.BlockSpec((part, 128), at),
            pl.BlockSpec(got.shape, lambda k: (0, 0, 0)),
            pl.BlockSpec((part, n), at),
            pl.BlockSpec((part, n), at),
        ],
        out_specs=[pair, pair, pair, pair],
        out_shape=[jax.ShapeDtypeStruct((2, rows // 4, n), F32)] * 4,
        scratch_shapes=[pltpu.VMEM((n, wide), F32), pltpu.VMEM((n, wide), F32)],
        compiler_params=pltpu.CompilerParams(vmem_limit_bytes=VMEM_LIMIT),
        name="basis_grads",
    )(me, cum, x, g, col, got, db1, dc1)


def row_kernel(first, count, x_ref, b_ref, c_ref, cum_ref, step_ref, col_ref, g_ref,
               s_ref, a_ref, got_ref, dx1_ref, q_ref, r_ref, *rest):
    dx_ref, dstep_ref, ddecay_ref, s0, a0 = rest[-5:]
    heads = cum_ref.shape[0]
    width = x_ref.shape[1] // heads
    k = first + pl.program_id(0)

    @pl.when(pl.program_id(0) == 0)
    def _():
        unpack(got_ref, s0, a0)

    before, after, own = totals(cum_ref, k)
    state = s_ref[0].astype(F32) + spread(jnp.exp(before), width) * s0[...]
    adj = a_ref[0].astype(F32) + spread(jnp.exp(after), width) * a0[...]
    carried = mm(c_ref[...], state.astype(BF16), 1, 0)
    fed = mm(b_ref[...], adj.astype(BF16), 1, 0)
    inflow = []
    lane = lax.broadcasted_iota(jnp.int32, (L, 128), 1)
    packed = r_ref[...]
    for h in range(heads):
        cs = slice(h * width, (h + 1) * width)
        ts = col_ref[:, 2 * heads + h : 2 * heads + h + 1]
        ds = fed[:, cs]
        dx_ref[:, cs] = (dx1_ref[:, cs].astype(F32) + ds * ts).astype(BF16)
        a = jnp.sum(x_ref[:, cs].astype(F32) * ds, axis=1, keepdims=True)
        q = jnp.sum(g_ref[:, cs].astype(F32) * carried[:, cs], axis=1, keepdims=True)
        packed = jnp.where(lane == h, a, packed)
        packed = jnp.where(lane == heads + h, q, packed)
        inflow.append(jnp.sum(adj[:, cs] * state[:, cs], axis=0, keepdims=True))
    rows = packed.T
    at = k * L + lax.broadcasted_iota(jnp.int32, (heads, L), 1)
    live = (at < count[0]).astype(F32)
    cum = cum_ref[:, pl.ds(pl.multiple_of(k * L, L), L)]
    more = jnp.exp(own - cum) * rows[0:heads]
    mine = step_ref[...] * live * more
    flow = jnp.sum(jnp.concatenate(inflow, axis=0), axis=1, keepdims=True) * jnp.exp(own)
    flow = flow + jnp.sum(mine, axis=1, keepdims=True)
    paid = jnp.exp(cum) * live * rows[heads : 2 * heads]
    dcum = q_ref[...] + paid - rows[2 * heads : 3 * heads] - mine
    ddecay_ref[...] = (running(dcum, True) + flow) * live
    dstep_ref[...] = (rows[3 * heads : 4 * heads] + more) * live


def row_grads(first, blocks, count, x, b, c, cum, step, col, g, s, a, got, dx1, q, r, earlier):
    heads, rows = cum.shape
    n = b.shape[1]
    wide = x.shape[1]
    at = lambda k: (first + k, 0)
    side = lambda k: (0, first + k)
    layer = pl.BlockSpec((1, n, wide), lambda k: (first + k, 0, 0))
    args = [count, x, b, c, cum, step, col, g, s, a, got, dx1, q, r]
    specs = [
        pl.BlockSpec(memory_space=pltpu.SMEM),
        pl.BlockSpec((L, wide), at),
        pl.BlockSpec((L, n), at),
        pl.BlockSpec((L, n), at),
        pl.BlockSpec((heads, rows), lambda k: (0, 0)),
        pl.BlockSpec((heads, L), side),
        pl.BlockSpec((L, 128), at),
        pl.BlockSpec((L, wide), at),
        layer,
        layer,
        pl.BlockSpec(got.shape, lambda k: (0, 0, 0)),
        pl.BlockSpec((L, wide), at),
        pl.BlockSpec((heads, L), lambda k: (0, first + k)),
        pl.BlockSpec((L, 128), at),
    ]
    alias = {}
    for i, v in enumerate(earlier):
        alias[len(args)] = i
        args.append(v)
        specs.append(pl.BlockSpec(memory_space=pl.ANY))

    def kernel(*refs):
        row_kernel(first, *refs)

    return pl.pallas_call(
        kernel,
        grid=(blocks,),
        in_specs=specs,
        out_specs=[
            pl.BlockSpec((L, wide), at),
            pl.BlockSpec((heads, L), side),
            pl.BlockSpec((heads, L), side),
        ],
        out_shape=[
            jax.ShapeDtypeStruct((rows, wide), BF16),
            jax.ShapeDtypeStruct((heads, rows), F32),
            jax.ShapeDtypeStruct((heads, rows), F32),
        ],
        scratch_shapes=[pltpu.VMEM((n, wide), F32), pltpu.VMEM((n, wide), F32)],
        input_output_aliases=alias,
        compiler_params=pltpu.CompilerParams(vmem_limit_bytes=VMEM_LIMIT),
        name="row_grads",
    )(*args)


def up(v):
    return lax.ppermute(v, "tp", [(i, (i + 1) % 4) for i in range(4)])


def down(v):
    return lax.ppermute(v, "tp", [(i, (i + 3) % 4) for i in range(4)])


def shards(x, b, c, step, decay, gain, count, g):
    devices = lax.axis_size("ctx")
    blocks = x.shape[0] // L
    me = lax.axis_index("tp")
    mine = me.astype(jnp.int32).reshape(1)
    cum, col, s, a, send = local_states(count, x, g, b, c, step, decay, devices)
    got = lax.all_to_all(send, "ctx", 0, 0, tiled=True)
    inner = within(gain, x, g, b, c, cum, col, s, a, 0, blocks // 2, ())
    got, inner = lax.optimization_barrier((got, inner))
    out = scan_devices(got)
    got = lax.all_to_all(out, "ctx", 0, 0, tiled=True)
    inner = within(gain, x, g, b, c, cum, col, s, a, blocks // 2, blocks // 2, inner)
    got, inner = lax.optimization_barrier((got, inner))
    dx1, db1, dc1, q, r = inner
    up1, down1, mid, own = basis_grads(mine, cum, x, g, col, got, db1, dc1)
    rows = lambda first, number, state, before: row_grads(
        first, number, count, x, b, c, cum, step, col, g, state, a, got, dx1, q, r, before
    )
    u, d = up(up1), down(down1)
    done = rows(0, FIRST, s, ())
    u, d, state, done = lax.optimization_barrier((u, d, s, done))
    p, w = up(u[0] + mid[0]), down(d[0] + mid[1])
    own = jnp.stack([own[0] + d[1] + p, own[1] + u[1] + w])
    own, state, done = lax.optimization_barrier((own, state, done))
    below, above = up(own), down(own)
    done = rows(FIRST, blocks - FIRST, state, done)
    below, above, done = lax.optimization_barrier((below, above, done))
    dx, dstep, ddecay = done
    far = (up(below[0]), down(above[1]))
    db = jnp.zeros((4, b.shape[0] // 4, b.shape[1]), F32)
    dc = db
    for k, v in ((0, own), (3, below), (1, above), (2, far)):
        at = ((me + k) % 4, 0, 0)
        db = lax.dynamic_update_slice(db, v[0][None], at)
        dc = lax.dynamic_update_slice(dc, v[1][None], at)
    return dx, db.reshape(b.shape), dc.reshape(c.shape), dstep, ddecay


def solution(mesh):
    placed = (
        P("ctx", "tp"), P("ctx", None), P("ctx", None), P("tp", "ctx"),
        P("tp", "ctx"), P("tp"), P("ctx"), P("ctx", "tp"),
    )
    return jax.shard_map(
        shards,
        mesh=mesh,
        in_specs=placed,
        out_specs=(P("ctx", "tp"), P("ctx", None), P("ctx", None), P("tp", "ctx"), P("tp", "ctx")),
        check_vma=False,
    )
```
